128 devices in a mesh: seg: 4 (over y), expert: 32 (over x, z, core).
Axes of the slice: x: 4, y: 4, z: 4, core: 2. Of those that a mesh axis runs over, the one named last changes fastest.
Arguments:
- frames: bfloat16 [32768, 1536], P(('seg', 'expert')), may hold values from -6 to 6
- expert_ids: int32 [32768, 2], P(('seg', 'expert')), may hold values from 0 to 31, all different within a row; in each aligned block of 256 rows (0 to 255, 256 to 511, ...) at most 24 rows name the same one
- gate_weights: float32 [32768, 2], P(('seg', 'expert')), may hold values from 0.2 to 1
- up_weight: bfloat16 [32, 1536, 2048], P('expert'), may hold values from -0.15625 to 0.15625
- down_weight: bfloat16 [32, 2048, 1536], P('expert'), may hold values from -0.125 to 0.125
- out_weight: bfloat16 [1536, 64], replicated, may hold values from -0.15625 to 0.15625
- in_conv: bfloat16 [7, 64, 2048], replicated, may hold values from -0.25 to 0.25
- snake_first: float32 [2048], replicated, may hold values from 0.5 to 2
- first_up: bfloat16 [16, 2048, 512], P(None, None, 'seg'), may hold values from -0.09375 to 0.09375
Outputs:
- features: float32 [4, 65536, 512], P(None, 'expert', 'seg')
The draws below stay inside these ranges and needn't reach their ends.
Inputs may be any that keep to these rules, and one draw needn't show every extreme that they name: `expert_ids`: in each aligned block of 256 rows (the rows of one device) no expert is named by more than 24 of the block's choices, and some block reaches 24; the two ids of a token differ.
All inputs are finite; a program needn't handle non-finite values.
Results may differ from the reference program's by a relative error of at most 0.005.
Values may be sent and summed in bfloat16 or wider, within the bound.
A program may use at most 128 MiB of HBM per device.

```python
import math
import jax
import jax.numpy as jnp
import numpy as np
from jax import lax

D = 1536
HID = 2048
LAT = 64
C1 = 2048
C2 = 512
TOK_DEV = 256
EXPERTS = 32
CAP = 24
SEQ_LEN = 8192
TOKENS = 32768
N_SEG = 4


def shard_levels(rng, extent, shards, low, largest):
    loudness, own = 1.0, jax.random.fold_in(rng, 6)
    for position, blocks in shards:
        steps = jnp.exp(jax.random.uniform(jax.random.fold_in(own, position), (blocks,), jnp.float32, low / len(shards), largest / len(shards)))
        loudness = loudness * jnp.repeat(steps, extent[position] // blocks).reshape([-1 if axis == position else 1 for axis in range(len(extent))])
    return loudness


def deal_out(stream_key, own, number, rows, number_of, top, limit, lean):
    ranking = jax.random.permutation(stream_key, number_of)
    crowded, usual = portions_of(number_of, rows * top, limit, lean, True), portions_of(number_of, rows * top, limit, lean, False)
    places = jnp.arange(number_of)

    def named(lengths, turn):
        used = int((lengths > 0).sum())
        fixed = max(1, used // 4)
        shifted = fixed + (places - fixed + turn * (used - fixed)) % max(1, number_of - fixed)
        return jnp.zeros((number_of,), jnp.int32).at[ranking[jnp.where(places < fixed, places, shifted)]].set(jnp.asarray(lengths, jnp.int32))

    lengths = jnp.where(number % 4 == 0, named(crowded, number // 4), named(usual, number - number // 4 - 1))
    mixed = jax.random.permutation(jax.random.fold_in(own, 3), number_of)
    donor, receiver = mixed[0:number_of // 2 * 2:2], mixed[1:number_of // 2 * 2:2]
    margin = jnp.minimum(lengths[donor] - 1, limit - lengths[receiver]) // 2
    margin = jnp.where((donor == ranking[0]) | (receiver == ranking[0]) | (lengths[receiver] == 0), 0, jnp.maximum(margin, 0))
    shifted = jax.random.randint(jax.random.fold_in(own, 4), (number_of // 2,), 0, 1 << 20) % (margin + 1)
    lengths = lengths.at[donor].add(-shifted).at[receiver].add(shifted)
    labels = jnp.searchsorted(jnp.cumsum(lengths), jnp.arange(rows * top), side="right").astype(jnp.int32)
    table = labels.reshape(top, rows).T
    table = table[jax.random.permutation(jax.random.fold_in(own, 1), rows)]
    turn = jax.random.randint(jax.random.fold_in(own, 2), (rows, 1), 0, top)
    return jnp.take_along_axis(table, (jnp.arange(top)[None, :] + turn) % top, axis=1)


def portions_of(number_of, total, bound, skew, full):
    portions = [(1 << 20) // math.isqrt(rank ** skew) + 1 for rank in range(1, number_of + 1)]
    largest = bound if full else min(bound, max(-(-total // number_of), total * portions[0] // sum(portions)))
    least = 1 if total - largest >= number_of - 1 else 0
    holding, surplus = [largest] + [least] * (number_of - 1), total - largest - least * (number_of - 1)
    while surplus > 0:
        free = [i for i in range(1, number_of) if holding[i] < largest] or [i for i in range(1, number_of) if holding[i] < bound]
        mass, left = sum([portions[i] for i in free]), surplus
        for i in free:
            extra = min(bound - holding[i], max(1, left * portions[i] // mass), surplus)
            holding[i] = holding[i] + extra
            surplus = surplus - extra
    return np.array(holding)


def scatter_about(rng, dims, width, bound, shards=(), kind=jnp.bfloat16):
    entries = jax.random.normal(rng, dims, jnp.float32) * width
    if len(shards) > 0:
        entries = shard_levels(rng, dims, shards, -0.22, 0.18) * entries
    return jnp.clip(entries, min=-bound, max=bound).astype(kind)


def setup_inputs(seed: int = 0) -> dict:
    splits = jax.random.split(jax.random.key(seed), 10)
    frames = scatter_about(splits[0], (TOKENS, D), 1.0, 6.0, ((0, 128),))
    expert_ids_keys = jax.random.split(jax.random.fold_in(splits[1], 1), TOKENS // TOK_DEV)
    expert_ids_turns = jax.random.permutation(jax.random.fold_in(splits[1], 3), TOKENS // TOK_DEV)
    expert_ids = jax.vmap(lambda own, number: deal_out(jax.random.fold_in(splits[1], 2), own, number, TOK_DEV, EXPERTS, 2, CAP, 2))(expert_ids_keys, expert_ids_turns).reshape((TOKENS, 2))
    gate_weights = jnp.clip(0.2 + 0.8 * jax.random.uniform(splits[2], (TOKENS, 2), jnp.float32) ** shard_levels(splits[2], (TOKENS, 2), ((0, 128),), -0.2, 0.2), 0.2, 1.0)
    up_weight = scatter_about(splits[3], (EXPERTS, D, HID), D ** -0.5, 0.15625, ((0, 32),))
    down_weight = scatter_about(splits[4], (EXPERTS, HID, D), HID ** -0.5, 0.125, ((0, 32),))
    out_weight = scatter_about(splits[5], (D, LAT), D ** -0.5, 0.15625)
    in_conv = scatter_about(splits[6], (7, LAT, C1), (7 * LAT) ** -0.5, 0.25)
    snake_first = jnp.clip(jnp.exp(jax.random.uniform(splits[7], (C1,), jnp.float32, math.log(0.5), math.log(2.0))), 0.5, 2.0)
    first_up = scatter_about(splits[8], (16, C1, C2), (2 * C1) ** -0.5, 0.09375, ((2, 4),))
    return dict(frames=frames, expert_ids=expert_ids, gate_weights=gate_weights, up_weight=up_weight, down_weight=down_weight, out_weight=out_weight, in_conv=in_conv, snake_first=snake_first, first_up=first_up)


def snake_act(values, alpha_row):
    return values + jnp.sin(alpha_row * values) ** 2 / alpha_row


def conv_seven(values, weights):
    length = values.shape[0]
    padded = jnp.pad(values, ((3, 3), (0, 0)))
    total = jnp.zeros((length, weights.shape[2]), jnp.float32)
    for tap_index in range(7):
        window = lax.slice_in_dim(padded, tap_index, tap_index + length, axis=0)
        total = total + jnp.dot(window, weights[tap_index], preferred_element_type=jnp.float32)
    return total


def upsample(values, weights):
    length = values.shape[0]
    padded = jnp.pad(values, ((1, 1), (0, 0))).astype(jnp.float32)
    wide = weights.astype(jnp.float32)
    prev_rows = padded[0:length]
    here_rows = padded[1:length + 1]
    next_rows = padded[2:length + 2]
    middle = jnp.einsum("lc,rco->lro", here_rows, wide[4:12])
    early_part = jnp.einsum("lc,rco->lro", prev_rows, wide[12:16])
    later_part = jnp.einsum("lc,rco->lro", next_rows, wide[0:4])
    joined = middle + jnp.concatenate([early_part, later_part], axis=1)
    return joined.reshape(length * 8, weights.shape[2])


def reference(frames, expert_ids, gate_weights, up_weight, down_weight, out_weight, in_conv, snake_first, first_up):
    devices_total = TOKENS // TOK_DEV
    flat_ids = expert_ids.reshape(devices_total, 2 * TOK_DEV)
    one_hot = (flat_ids[:, :, None] == jnp.arange(EXPERTS, dtype=jnp.int32)[None, None, :]).astype(jnp.int32)
    before = jnp.cumsum(one_hot, axis=1) - one_hot
    slot_pos = jnp.sum(before * one_hot, axis=2)
    dest_index = flat_ids * CAP + slot_pos
    local_index = jnp.arange(2 * TOK_DEV, dtype=jnp.int32)
    device_index = jnp.arange(devices_total, dtype=jnp.int32)
    global_index = device_index[:, None] * (2 * TOK_DEV) + local_index[None, :]
    table = jnp.full((devices_total, EXPERTS * CAP), -1, jnp.int32)
    table = table.at[device_index[:, None], dest_index].set(global_index)
    flat_gates = gate_weights.reshape(-1)

    def one_expert(carry, expert_index):
        assigned = lax.dynamic_slice_in_dim(table, expert_index * CAP, CAP, axis=1).reshape(-1)
        present = assigned >= 0
        safe_index = jnp.where(present, assigned, 0)
        token_index = safe_index // 2
        rows_in = frames[token_index]
        hidden_units = jax.nn.gelu(jnp.dot(rows_in, up_weight[expert_index], preferred_element_type=jnp.float32), approximate=True).astype(jnp.bfloat16)
        expert_out = jnp.dot(hidden_units, down_weight[expert_index], preferred_element_type=jnp.float32).astype(jnp.bfloat16)
        projected = jnp.dot(expert_out, out_weight, preferred_element_type=jnp.float32)
        weighting = jnp.where(present, flat_gates[safe_index], jnp.zeros_like(flat_gates[safe_index]))
        carry = carry.at[token_index].add(projected * weighting[:, None])
        return carry, None

    base = jnp.dot(frames, out_weight, preferred_element_type=jnp.float32)
    latent, _ = lax.scan(one_expert, base, jnp.arange(EXPERTS, dtype=jnp.int32))
    latent_low = latent.astype(jnp.bfloat16)
    results = []
    for sequence in range(N_SEG):
        rows = latent_low[sequence * SEQ_LEN:(sequence + 1) * SEQ_LEN]
        first_in = conv_seven(rows, in_conv)
        act_first = snake_act(first_in, snake_first).astype(jnp.bfloat16)
        results.append(upsample(act_first, first_up))
    return jnp.stack(results, axis=0)
```

```python
import jax
import jax.numpy as jnp
from jax import lax
from jax.sharding import PartitionSpec as P

SIN2 = (
    9.869604110717773,
    -32.469669342041016,
    42.727195739746094,
    -30.101465225219727,
    13.05009937286377,
    -3.3565926551818848,
)
PI_INV = 0.3183098861837907


def snake_act(values, freq, inv_alpha):
    turns = values * freq
    frac = turns - jnp.round(turns)
    t = frac * frac
    q = jnp.float32(SIN2[5])
    for coef in SIN2[4::-1]:
        q = q * t + coef
    return values + jnp.minimum(q * t, 1.0) * inv_alpha


def edge_rows(value, width):
    size = lax.axis_size("expert")
    up = [(i, (i + 1) % size) for i in range(size - 1)]
    down = [(j, i) for i, j in up]
    before = lax.ppermute(value[-width:], "expert", up)
    after = lax.ppermute(value[:width], "expert", down)
    return jnp.concatenate([before, value, after], axis=0)


def conv_seven(padded, weights, length):
    windows = [lax.slice_in_dim(padded, tap, tap + length, axis=1) for tap in range(7)]
    stacked = jnp.concatenate(windows, axis=2)
    return jnp.einsum(
        "klc,co->klo",
        stacked,
        weights.reshape(-1, weights.shape[2]),
        preferred_element_type=jnp.float32,
    )


def upsample(padded, weights, length):
    prev_rows = padded[:, 0:length]
    here_rows = padded[:, 1 : length + 1]
    next_rows = padded[:, 2 : length + 2]
    middle = jnp.einsum(
        "klc,rco->klro", here_rows, weights[4:12], preferred_element_type=jnp.float32
    )
    early_part = jnp.einsum(
        "klc,rco->klro", prev_rows, weights[12:16], preferred_element_type=jnp.float32
    )
    later_part = jnp.einsum(
        "klc,rco->klro", next_rows, weights[0:4], preferred_element_type=jnp.float32
    )
    joined = middle + jnp.concatenate([early_part, later_part], axis=2)
    return joined.reshape(padded.shape[0], length * 8, weights.shape[2])


def local(
    frames,
    expert_ids,
    gate_weights,
    up_weight,
    down_weight,
    out_weight,
    in_conv,
    snake_first,
    first_up,
):
    tok_rows, model_dim = frames.shape
    num_experts = lax.axis_size("expert")
    capacity = 3 * tok_rows // num_experts
    lat_dim = out_weight.shape[1]

    experts = jnp.arange(num_experts, dtype=jnp.int32)[:, None]
    first = expert_ids[:, 0][None, :] == experts
    second = expert_ids[:, 1][None, :] == experts
    named = first | second
    row = jnp.arange(tok_rows, dtype=jnp.int32)
    earlier = (row[:, None] < row[None, :]).astype(jnp.bfloat16)
    rank = jnp.dot(named.astype(jnp.bfloat16), earlier, preferred_element_type=jnp.float32)
    slots = jnp.arange(capacity, dtype=jnp.int32).astype(jnp.float32)
    pick = (rank[:, None, :] == slots[None, :, None]) & named[:, None, :]
    gates = jnp.where(first, gate_weights[:, 0][None, :], 0.0) + jnp.where(
        second, gate_weights[:, 1][None, :], 0.0
    )
    weighted = jnp.where(pick, gates[:, None, :], 0.0).reshape(-1, tok_rows)

    send = jnp.dot(
        pick.reshape(-1, tok_rows).astype(jnp.bfloat16), frames, preferred_element_type=jnp.float32
    ).astype(jnp.bfloat16)
    send = send.reshape(num_experts, capacity, model_dim)
    received = lax.all_to_all(send, "expert", split_axis=0, concat_axis=0, tiled=True)
    flat_rows = received.reshape(-1, model_dim)
    hidden_units = jax.nn.gelu(
        jnp.dot(flat_rows, up_weight[0], preferred_element_type=jnp.float32), approximate=True
    ).astype(jnp.bfloat16)
    expert_out = jnp.dot(hidden_units, down_weight[0], preferred_element_type=jnp.float32).astype(
        jnp.bfloat16
    )
    projected = jnp.dot(expert_out, out_weight, preferred_element_type=jnp.float32)
    projected = projected.reshape(num_experts, capacity, lat_dim)
    returned = lax.all_to_all(projected, "expert", split_axis=0, concat_axis=0, tiled=True)
    gated = lax.dot_general(
        weighted,
        returned.reshape(-1, lat_dim),
        (((0,), (0,)), ((), ())),
        precision=lax.Precision.HIGHEST,
        preferred_element_type=jnp.float32,
    )
    latent = jnp.dot(frames, out_weight, preferred_element_type=jnp.float32) + gated
    latent_low = latent.astype(jnp.bfloat16)

    padded = edge_rows(latent_low, 4)
    num_seg = lax.axis_size("seg")
    spread = jnp.broadcast_to(padded[None], (num_seg,) + padded.shape)
    sequences = lax.all_to_all(spread, "seg", split_axis=0, concat_axis=0, tiled=True)
    first_in = conv_seven(sequences, in_conv, tok_rows + 2)
    act_first = snake_act(first_in, snake_first * PI_INV, 1.0 / snake_first)
    slab = lax.axis_index("expert")
    frame = slab * tok_rows - 1 + jnp.arange(tok_rows + 2, dtype=jnp.int32)
    inside = (frame >= 0) & (frame < num_experts * tok_rows)
    act_first = jnp.where(inside[None, :, None], act_first, 0.0).astype(jnp.bfloat16)
    return upsample(act_first, first_up, tok_rows)


def solution(mesh):
    placed = (
        P(("seg", "expert"), None),
        P(("seg", "expert"), None),
        P(("seg", "expert"), None),
        P("expert", None, None),
        P("expert", None, None),
        P(),
        P(),
        P(),
        P(None, None, "seg"),
    )
    return jax.shard_map(
        local, mesh=mesh, in_specs=placed, out_specs=P(None, "expert", "seg"), check_vma=False
    )
```

```python
import jax
import jax.numpy as jnp
from jax import lax
from jax.experimental import pallas as pl
from jax.experimental.pallas import tpu as pltpu
from jax.sharding import PartitionSpec as P

SIN2 = (
    9.869604110717773,
    -32.469669342041016,
    42.727195739746094,
    -30.101465225219727,
    13.05009937286377,
    -3.3565926551818848,
)
PI_INV = 0.3183098861837907
SEQS = 4


def snake(values, freq, inv_alpha):
    turns = values * freq
    frac = turns - jnp.round(turns)
    t = frac * frac
    q = jnp.float32(SIN2[5])
    for coef in SIN2[4::-1]:
        q = q * t + coef
    return values + jnp.minimum(q * t, 1.0) * inv_alpha


def edge_rows(value, width):
    size = lax.axis_size("expert")
    up = [(i, (i + 1) % size) for i in range(size - 1)]
    down = [(j, i) for i, j in up]
    before = lax.ppermute(value[-width:], "expert", up)
    after = lax.ppermute(value[:width], "expert", down)
    return jnp.concatenate([before, value, after], axis=0)


def decode_kernel(
    main_ref, edge_ref, freq_ref, inv_ref, conv_hbm, up_hbm, out_hbm,
    plain, pairs, cols, rims, wide, act, here, other, tile, conv_w, up_w, in_sems, out_sems,
):
    rows = main_ref.shape[1] * 2
    total = SEQS * rows
    get_conv = pltpu.make_async_copy(conv_hbm, conv_w.at[pl.ds(0, 448)], in_sems.at[0])
    get_conv.start()
    get_up = pltpu.make_async_copy(up_hbm, up_w, in_sems.at[1])
    get_up.start()
    slab = lax.axis_index("expert")
    keep_left = jnp.where(slab == 0, 0.0, 1.0)
    keep_right = jnp.where(slab == lax.axis_size("expert") - 1, 0.0, 1.0)
    conv_w[pl.ds(448, 64), :] = jnp.zeros((64, conv_w.shape[1]), jnp.bfloat16)
    plain[...] = jnp.zeros_like(plain)
    rims[...] = jnp.zeros_like(rims)
    for s in range(SEQS):
        body = main_ref[s].astype(jnp.float32)
        half = rows // 2
        plain[pl.ds(8, half), 0:64] = body[:, 0:64]
        plain[pl.ds(8 + half, half), 0:64] = body[:, 64:128]
        plain[pl.ds(0, 8), 0:64] = edge_ref[s, 0][:, 0:64] * keep_left
        plain[pl.ds(8 + rows, 8), 0:64] = edge_ref[s, 1][:, 0:64] * keep_right
        pairs[...] = plain[pl.ds(0, rows + 16), :] + pltpu.roll(
            plain[pl.ds(1, rows + 16), :], 64, axis=1
        )
        for m in range(4):
            lanes = slice(128 * m, 128 * m + 128)
            cols[pl.ds(s * rows, rows), lanes] = pairs[pl.ds(5 + 2 * m, rows), :].astype(jnp.bfloat16)
            rims[pl.ds(2 * s, 1), lanes] = pairs[pl.ds(4 + 2 * m, 1), :]
            rims[pl.ds(2 * s + 1, 1), lanes] = pairs[pl.ds(5 + 2 * m + rows, 1), :]
    cols[pl.ds(total, 16), :] = rims[...].astype(jnp.bfloat16)
    get_conv.wait()

    @pl.loop(0, act.shape[1] // 256)
    def _(n):
        lanes = pl.ds(pl.multiple_of(n * 256, 256), 256)
        freq = freq_ref[:, lanes]
        inv = inv_ref[:, lanes]
        weight = conv_w[:, lanes]
        for part, size in [(s * rows, rows) for s in range(SEQS)] + [(total, 16)]:
            value = jnp.dot(
                cols[pl.ds(part, size), :], weight, preferred_element_type=jnp.float32
            )
            act[pl.ds(part, size), lanes] = snake(value, freq, inv).astype(jnp.bfloat16)

    line = lax.broadcasted_iota(jnp.int32, (16, 1), 0)
    gone = jnp.where(line % 2 == 0, keep_left, keep_right)
    edge_act = act[pl.ds(total, 16), :].astype(jnp.float32) * gone
    act[pl.ds(total, 16), :] = edge_act.astype(jnp.bfloat16)
    get_up.wait()

    for q in range(4):
        r = 2 * q
        tap = (r + 12) % 16
        near = jnp.concatenate([up_w[r + 4], up_w[r + 5]], axis=1)
        far = jnp.concatenate([up_w[tap], up_w[tap + 1]], axis=1)
        rim = jnp.dot(act[pl.ds(total, 16), :], far, preferred_element_type=jnp.float32)
        for s in range(SEQS):
            block = act[pl.ds(s * rows, rows), :]
            here[...] = jnp.dot(block, near, preferred_element_type=jnp.float32)
            other[pl.ds(8, rows), :] = jnp.dot(block, far, preferred_element_type=jnp.float32)
            if q < 2:
                other[pl.ds(7, 1), :] = rim[2 * s : 2 * s + 1]
                shifted = other[pl.ds(7, rows), :]
            else:
                other[pl.ds(8 + rows, 1), :] = rim[2 * s + 1 : 2 * s + 2]
                shifted = other[pl.ds(9, rows), :]
            both = here[...] + shifted
            tile[s, pl.ds(r, rows, stride=8), :] = both[:, 0:128]
            tile[s, pl.ds(r + 1, rows, stride=8), :] = both[:, 128:256]
    puts = [
        pltpu.make_async_copy(tile.at[s], out_hbm.at[s], out_sems.at[s]) for s in range(SEQS)
    ]
    for put in puts:
        put.start()
    for put in puts:
        put.wait()


def decode(main, edges, in_conv, snake_first, first_up):
    channels = in_conv.shape[2]
    rows = main.shape[1] * 2
    total = SEQS * rows + 16
    vmem = pl.BlockSpec(memory_space=pltpu.VMEM)
    anywhere = pl.BlockSpec(memory_space=pl.ANY)
    return pl.pallas_call(
        decode_kernel,
        out_shape=jax.ShapeDtypeStruct((SEQS, rows * 8, first_up.shape[2]), jnp.float32),
        in_specs=[vmem, vmem, vmem, vmem, anywhere, anywhere],
        out_specs=anywhere,
        scratch_shapes=[
            pltpu.VMEM((rows + 24, 128), jnp.float32),
            pltpu.VMEM((rows + 16, 128), jnp.float32),
            pltpu.VMEM((total, 512), jnp.bfloat16),
            pltpu.VMEM((16, 512), jnp.float32),
            pltpu.VMEM((8, 128), jnp.float32),
            pltpu.VMEM((total, channels), jnp.bfloat16),
            pltpu.VMEM((rows, 256), jnp.float32),
            pltpu.VMEM((rows + 16, 256), jnp.float32),
            pltpu.VMEM((SEQS, rows * 8, first_up.shape[2]), jnp.float32),
            pltpu.VMEM((512, channels), jnp.bfloat16),
            pltpu.VMEM(first_up.shape, jnp.bfloat16),
            pltpu.SemaphoreType.DMA((2,)),
            pltpu.SemaphoreType.DMA((SEQS,)),
        ],
        compiler_params=pltpu.CompilerParams(vmem_limit_bytes=48 << 20),
        cost_estimate=pl.CostEstimate(flops=11 * 10**9, bytes_accessed=16 << 20, transcendentals=0),
        name="decode",
    )(
        main,
        edges,
        (snake_first * PI_INV)[None, :],
        (1.0 / snake_first)[None, :],
        in_conv.reshape(-1, channels),
        first_up,
    )


def local(
    frames,
    expert_ids,
    gate_weights,
    up_weight,
    down_weight,
    out_weight,
    in_conv,
    snake_first,
    first_up,
):
    tok_rows, model_dim = frames.shape
    num_experts = lax.axis_size("expert")
    capacity = 3 * tok_rows // num_experts
    lat_dim = out_weight.shape[1]

    experts = jnp.arange(num_experts, dtype=jnp.int32)[:, None]
    first = expert_ids[:, 0][None, :] == experts
    second = expert_ids[:, 1][None, :] == experts
    named = first | second
    row = jnp.arange(tok_rows, dtype=jnp.int32)
    earlier = (row[:, None] < row[None, :]).astype(jnp.bfloat16)
    rank = jnp.dot(named.astype(jnp.bfloat16), earlier, preferred_element_type=jnp.float32)
    slots = jnp.arange(capacity, dtype=jnp.int32).astype(jnp.float32)
    pick = (rank[:, None, :] == slots[None, :, None]) & named[:, None, :]
    gates = jnp.where(first, gate_weights[:, 0][None, :], 0.0) + jnp.where(
        second, gate_weights[:, 1][None, :], 0.0
    )
    weighted = jnp.where(pick, gates[:, None, :], 0.0).reshape(-1, tok_rows)

    send = jnp.dot(
        pick.reshape(-1, tok_rows).astype(jnp.bfloat16), frames, preferred_element_type=jnp.float32
    ).astype(jnp.bfloat16)
    send = send.reshape(num_experts, capacity, model_dim)
    received = lax.all_to_all(send, "expert", split_axis=0, concat_axis=0, tiled=True)
    flat_rows = received.reshape(-1, model_dim)
    hidden_units = jax.nn.gelu(
        jnp.dot(flat_rows, up_weight[0], preferred_element_type=jnp.float32), approximate=True
    ).astype(jnp.bfloat16)
    expert_out = jnp.dot(hidden_units, down_weight[0], preferred_element_type=jnp.float32).astype(
        jnp.bfloat16
    )
    projected = jnp.dot(expert_out, out_weight, preferred_element_type=jnp.float32)
    projected = projected.reshape(num_experts, capacity, lat_dim)
    returned = lax.all_to_all(projected, "expert", split_axis=0, concat_axis=0, tiled=True)
    gated = lax.dot_general(
        weighted,
        returned.reshape(-1, lat_dim),
        (((0,), (0,)), ((), ())),
        precision=lax.Precision.HIGHEST,
        preferred_element_type=jnp.float32,
    )
    latent = jnp.dot(frames, out_weight, preferred_element_type=jnp.float32) + gated
    latent_low = latent.astype(jnp.bfloat16)

    padded = edge_rows(latent_low, 4)
    num_seg = lax.axis_size("seg")
    spread = jnp.broadcast_to(padded[None], (num_seg,) + padded.shape)
    sequences = lax.all_to_all(spread, "seg", split_axis=0, concat_axis=0, tiled=True)
    half = tok_rows // 2
    main = jnp.concatenate([sequences[:, 4 : 4 + half], sequences[:, 4 + half : 4 + tok_rows]], axis=2)
    left = jnp.pad(sequences[:, 0:4], ((0, 0), (4, 0), (0, 64)))
    right = jnp.pad(sequences[:, 4 + tok_rows :], ((0, 0), (0, 4), (0, 64)))
    edges = jnp.stack([left, right], axis=1).astype(jnp.float32)
    return decode(main, edges, in_conv, snake_first, first_up)


def solution(mesh):
    placed = (
        P(("seg", "expert"), None),
        P(("seg", "expert"), None),
        P(("seg", "expert"), None),
        P("expert", None, None),
        P("expert", None, None),
        P(),
        P(),
        P(),
        P(None, None, "seg"),
    )
    return jax.shard_map(
        local, mesh=mesh, in_specs=placed, out_specs=P(None, "expert", "seg"), check_vma=False
    )
```

```python
import jax
import jax.numpy as jnp
from jax import lax
from jax.experimental import pallas as pl
from jax.experimental.pallas import tpu as pltpu
from jax.sharding import PartitionSpec as P

SIN2 = (
    9.869604110717773,
    -32.469669342041016,
    42.727195739746094,
    -30.101465225219727,
    13.05009937286377,
    -3.3565926551818848,
)
PI_INV = 0.3183098861837907
SEQS = 4
SIDE = 4


def snake(values, freq, inv_alpha):
    turns = values * freq
    frac = turns - jnp.round(turns)
    t = frac * frac
    q = jnp.float32(SIN2[5])
    for coef in SIN2[4::-1]:
        q = q * t + coef
    return values + jnp.minimum(q * t, 1.0) * inv_alpha


def distance(step):
    return min(step[0], SIDE - step[0]) + min(step[1], SIDE - step[1])


OFFSETS = [(0, 0, 0), (0, 0, 1)] + sorted(
    [
        (dx, dz, dc)
        for dx in range(SIDE)
        for dz in range(SIDE)
        for dc in range(2)
        if (dx, dz) != (0, 0)
    ],
    key=lambda step: (-distance(step), step[2]),
)
GROUPS = ((0, 10), (10, 20), (20, 28), (28, 32))
PACKS = (8, 16, 24, 32)
MESH = pl.DeviceIdType.MESH


def gelu(v):
    return 0.5 * v * (1.0 + jnp.tanh(0.7978845608 * (v + 0.044715 * v * v * v)))


def expert_kernel(
    frames_hbm, ids_hbm, gates_hbm, proj_hbm, up_hbm, down_hbm,
    main_ref, edge_ref,
    frames, ids, gates, proj, ranks, send, recv, rows_in, hidden, up_w, down_w, proj_w, table,
    picks, base, answer, returned, packed, ends, main_buf, edge_buf,
    w_sems, self_sem, out_s, out_r, back_s, back_r, main_s, main_r, end_s, end_r,
):
    expert = lax.axis_index("expert")
    seg = lax.axis_index("seg")
    x, z, core = expert // (2 * SIDE), (expert // 2) % SIDE, expert % 2

    def toward(step):
        dx, dz, dc = step
        return (((x + dx) % SIDE) * SIDE + (z + dz) % SIDE) * 2 + (core + dc) % 2

    def away(step):
        dx, dz, dc = step
        return (((x + SIDE - dx) % SIDE) * SIDE + (z + SIDE - dz) % SIDE) * 2 + (core + dc) % 2

    count = len(OFFSETS)
    sides = ((expert + 1) % count, (expert + count - 1) % count)
    barrier = pltpu.get_barrier_semaphore()
    for step in OFFSETS[1:]:
        pl.semaphore_signal(barrier, inc=1, device_id={"expert": toward(step)}, device_id_type=MESH)
    for ds in range(1, SEQS):
        for to in (expert,) + sides:
            pl.semaphore_signal(
                barrier,
                inc=1,
                device_id={"seg": (seg + ds) % SEQS, "expert": to},
                device_id_type=MESH,
            )
    gets = [
        pltpu.make_async_copy(src, dst, w_sems.at[k])
        for k, (src, dst) in enumerate(
            [
                (ids_hbm, ids), (frames_hbm, frames), (gates_hbm, gates), (proj_hbm, proj),
                (up_hbm, up_w), (down_hbm, down_w),
            ]
        )
    ]
    for get in gets:
        get.start()

    tokens, dim = frames.shape
    slots = recv.shape[1]
    gets[0].wait()
    name = lax.broadcasted_iota(jnp.int32, (count, tokens), 0)
    named = (ids[0:1, :] == name) | (ids[1:2, :] == name)
    line = lax.broadcasted_iota(jnp.int32, (tokens, tokens), 0)
    across = lax.broadcasted_iota(jnp.int32, (tokens, tokens), 1)
    earlier = jnp.where(line < across, 1.0, 0.0).astype(jnp.bfloat16)
    rank = jnp.dot(
        jnp.where(named, 1.0, 0.0).astype(jnp.bfloat16), earlier, preferred_element_type=jnp.float32
    )
    ranks[...] = jnp.where(named, rank, -1.0)
    gets[1].wait()
    slot = lax.broadcasted_iota(jnp.int32, (slots, 1), 0).astype(jnp.float32)

    def pack(lo, hi):
        rows = [
            jnp.where(ranks[pl.ds(toward(OFFSETS[i]), 1), :] == slot, 1.0, 0.0) for i in range(lo, hi)
        ]
        chosen = jnp.concatenate(rows, axis=0).astype(jnp.bfloat16)
        for n in range(dim // 512):
            lanes = slice(512 * n, 512 * n + 512)
            value = jnp.dot(chosen, frames[:, lanes], preferred_element_type=jnp.float32)
            send[lo:hi, :, lanes] = value.astype(jnp.bfloat16).reshape(hi - lo, slots, 512)

    outs = [None] * count

    def dispatch(lo, hi):
        for i in range(lo, hi):
            if i == 0:
                outs[i] = pltpu.make_async_copy(send.at[0], recv.at[0], self_sem)
            else:
                outs[i] = pltpu.make_async_remote_copy(
                    src_ref=send.at[i],
                    dst_ref=recv.at[i],
                    send_sem=out_s.at[i],
                    recv_sem=out_r.at[i],
                    device_id={"expert": toward(OFFSETS[i])},
                    device_id_type=MESH,
                )
            outs[i].start()

    pack(0, PACKS[0])
    pl.semaphore_wait(barrier, count - 1 + 3 * (SEQS - 1))
    start = 0
    for lo, hi in zip(PACKS, PACKS[1:]):
        dispatch(start, lo)
        pack(lo, hi)
        start = lo
    dispatch(start, count)

    gets[2].wait()
    gets[3].wait()
    lat = proj.shape[0]
    proj_w[0:lat, :] = proj[...]
    proj_w[lat : 2 * lat, :] = proj[...]
    base[...] = lax.dot_general(
        frames[...], proj_w[...], (((1,), (1,)), ((), ())), preferred_element_type=jnp.float32
    )
    table[...] = jnp.zeros_like(table)
    table[0:2, :] = ids[...].astype(jnp.float32)
    table[8:10, :] = gates[...]
    turned = jnp.transpose(table[...])
    choice = [turned[:, 0:1], turned[:, 1:2]]
    gate = [turned[:, 8:9], turned[:, 9:10]]
    lane = lax.broadcasted_iota(jnp.int32, (tokens, 128), 1).astype(jnp.float32)
    hits = [lane == choice[0], lane == choice[1]]
    named = jnp.where(hits[0] | hits[1], 1.0, 0.0).astype(jnp.bfloat16)
    before = jnp.where(across < line, 1.0, 0.0).astype(jnp.bfloat16)
    rank = jnp.dot(before, named, preferred_element_type=jnp.float32)
    spot = lax.broadcasted_iota(jnp.int32, (tokens, count * slots), 1).astype(jnp.float32)
    for c in range(2):
        dest = choice[c] * slots + jnp.sum(
            jnp.where(hits[c], rank, 0.0), axis=1, keepdims=True
        )
        picks[pl.ds(c * tokens, tokens), :] = jnp.where(spot == dest, 1.0, 0.0).astype(jnp.bfloat16)

    gets[4].wait()
    gets[5].wait()
    backs = [None] * count
    first = lax.broadcasted_iota(jnp.int32, (1, 2 * lat), 1) < lat
    width = 512
    for lo, hi in GROUPS:
        for i in range(lo, hi):
            if i == 0:
                outs[i].wait()
            else:
                outs[i].wait_recv()
        size = (hi - lo) * slots
        rows_in[0:size, :] = recv[lo:hi].reshape(size, recv.shape[2])

        @pl.loop(0, hidden.shape[1] // width)
        def _(n):
            lanes = pl.ds(pl.multiple_of(n * width, width), width)
            value = jnp.dot(
                rows_in[0:size, :], up_w[0, :, lanes], preferred_element_type=jnp.float32
            )
            hidden[0:size, lanes] = gelu(value).astype(jnp.bfloat16)

        sent = jnp.zeros((size, 2 * lat), jnp.float32)
        for n in range(rows_in.shape[1] // width):
            lanes = slice(n * width, n * width + width)
            value = jnp.dot(
                hidden[0:size, :], down_w[0, :, lanes], preferred_element_type=jnp.float32
            ).astype(jnp.bfloat16)
            sent = sent + lax.dot_general(
                value, proj_w[:, lanes], (((1,), (1,)), ((), ())), preferred_element_type=jnp.float32
            )
        high = sent.astype(jnp.bfloat16).astype(jnp.float32)
        split = jnp.where(first, high, sent - high).astype(jnp.bfloat16)
        answer[lo:hi] = split.reshape(hi - lo, slots, 2 * lat)
        for i in range(lo, hi):
            if i == 0:
                backs[i] = pltpu.make_async_copy(answer.at[i], returned.at[expert], back_r.at[i])
            else:
                backs[i] = pltpu.make_async_remote_copy(
                    src_ref=answer.at[i],
                    dst_ref=returned.at[expert],
                    send_sem=back_s.at[i],
                    recv_sem=back_r.at[i],
                    device_id={"expert": away(OFFSETS[i])},
                    device_id_type=MESH,
                )
            backs[i].start()

    for i in range(count):
        if i == 0:
            backs[i].wait()
        else:
            pltpu.make_async_remote_copy(
                src_ref=answer.at[i],
                dst_ref=returned.at[toward(OFFSETS[i])],
                send_sem=back_s.at[i],
                recv_sem=back_r.at[i],
                device_id={"expert": away(OFFSETS[i])},
                device_id_type=MESH,
            ).wait_recv()
    got = jnp.dot(
        picks[...],
        returned[...].reshape(count * slots, 2 * lat),
        preferred_element_type=jnp.float32,
    )
    got = got + pltpu.roll(got, lat, axis=1)
    latent = base[...] + gate[0] * got[0:tokens] + gate[1] * got[tokens:]
    latent = latent.astype(jnp.bfloat16).astype(jnp.float32)
    half = tokens // 2
    packed[...] = jnp.where(first, latent[0:half], latent[half:]).astype(jnp.bfloat16)
    ends[0] = latent[tokens - 8 :]
    ends[1] = latent[0:8]

    sends = []
    for side in range(2):
        for ds in range(SEQS):
            k = side * SEQS + ds
            copy = pltpu.make_async_remote_copy(
                src_ref=ends.at[side],
                dst_ref=edge_buf.at[seg, side],
                send_sem=end_s.at[k],
                recv_sem=end_r.at[k],
                device_id={"seg": (seg + ds) % SEQS, "expert": sides[side]},
                device_id_type=MESH,
            )
            copy.start()
            sends.append((copy, edge_buf.at[(seg + SEQS - ds) % SEQS, side], end_s.at[k], end_r.at[k]))
    for ds in range(1, SEQS):
        copy = pltpu.make_async_remote_copy(
            src_ref=packed,
            dst_ref=main_buf.at[seg],
            send_sem=main_s.at[ds],
            recv_sem=main_r.at[ds],
            device_id={"seg": (seg + ds) % SEQS, "expert": expert},
            device_id_type=MESH,
        )
        copy.start()
        sends.append((copy, main_buf.at[(seg + SEQS - ds) % SEQS], main_s.at[ds], main_r.at[ds]))
    main_buf[seg] = packed[...]
    for k, (copy, landing, ss, rs) in enumerate(sends):
        pltpu.make_async_remote_copy(
            src_ref=ends.at[0] if k < 2 * SEQS else packed,
            dst_ref=landing,
            send_sem=ss,
            recv_sem=rs,
            device_id={"seg": (seg + 1) % SEQS, "expert": expert},
            device_id_type=MESH,
        ).wait_recv()
    main_ref[...] = main_buf[...]
    edge_ref[...] = edge_buf[...]
    for copy in outs[1:] + backs[1:] + [entry[0] for entry in sends]:
        copy.wait_send()


def experts(frames, ids, gates, proj, up_weight, down_weight):
    tokens, dim = frames.shape
    count = len(OFFSETS)
    slots = 3 * tokens // count
    hid = up_weight.shape[2]
    lat = proj.shape[0]
    vmem = pl.BlockSpec(memory_space=pltpu.VMEM)
    anywhere = pl.BlockSpec(memory_space=pltpu.HBM)
    bf16, f32 = jnp.bfloat16, jnp.float32
    top = max(hi - lo for lo, hi in GROUPS) * slots
    sems = lambda *shape: pltpu.SemaphoreType.DMA(shape)
    return pl.pallas_call(
        expert_kernel,
        out_shape=(
            jax.ShapeDtypeStruct((SEQS, tokens // 2, 2 * lat), bf16),
            jax.ShapeDtypeStruct((SEQS, 2, 8, 2 * lat), f32),
        ),
        in_specs=[anywhere] * 6,
        out_specs=(vmem, vmem),
        scratch_shapes=[
            pltpu.VMEM(frames.shape, bf16),
            pltpu.VMEM(ids.shape, jnp.int32),
            pltpu.VMEM(gates.shape, f32),
            pltpu.VMEM(proj.shape, bf16),
            pltpu.VMEM((count, tokens), f32),
            pltpu.VMEM((count, slots, dim), bf16),
            pltpu.VMEM((count, slots, dim), bf16),
            pltpu.VMEM((top, dim), bf16),
            pltpu.VMEM((top, hid), bf16),
            pltpu.VMEM(up_weight.shape, bf16),
            pltpu.VMEM(down_weight.shape, bf16),
            pltpu.VMEM((2 * lat, dim), bf16),
            pltpu.VMEM((128, tokens), f32),
            pltpu.VMEM((2 * tokens, count * slots), bf16),
            pltpu.VMEM((tokens, 2 * lat), f32),
            pltpu.VMEM((count, slots, 2 * lat), bf16),
            pltpu.VMEM((count, slots, 2 * lat), bf16),
            pltpu.VMEM((tokens // 2, 2 * lat), bf16),
            pltpu.VMEM((2, 8, 2 * lat), f32),
            pltpu.VMEM((SEQS, tokens // 2, 2 * lat), bf16),
            pltpu.VMEM((SEQS, 2, 8, 2 * lat), f32),
            sems(6), sems(), sems(count), sems(count), sems(count), sems(count),
            sems(SEQS), sems(SEQS), sems(2 * SEQS), sems(2 * SEQS),
        ],
        compiler_params=pltpu.CompilerParams(
            collective_id=0, has_side_effects=True, vmem_limit_bytes=63 << 20
        ),
        cost_estimate=pl.CostEstimate(
            flops=10 * 10**9, bytes_accessed=16 << 20, transcendentals=0
        ),
        name="experts",
    )(frames, ids, gates, proj, up_weight, down_weight)


def decode_kernel(
    main_ref, edge_ref, alpha_ref, conv_hbm, up_hbm, out_hbm,
    plain, pairs, cols, rims, wide, act, here, other, tile, conv_w, up_w, in_sems, out_sems,
):
    rows = main_ref.shape[1] * 2
    total = SEQS * rows
    get_conv = pltpu.make_async_copy(conv_hbm, conv_w.at[pl.ds(0, 448)], in_sems.at[0])
    get_conv.start()
    get_up = pltpu.make_async_copy(up_hbm, up_w, in_sems.at[1])
    get_up.start()
    slab = lax.axis_index("expert")
    keep_left = jnp.where(slab == 0, 0.0, 1.0)
    keep_right = jnp.where(slab == lax.axis_size("expert") - 1, 0.0, 1.0)
    conv_w[pl.ds(448, 64), :] = jnp.zeros((64, conv_w.shape[1]), jnp.bfloat16)
    plain[...] = jnp.zeros_like(plain)
    rims[...] = jnp.zeros_like(rims)
    for s in range(SEQS):
        body = main_ref[s].astype(jnp.float32)
        half = rows // 2
        plain[pl.ds(8, half), 0:64] = body[:, 0:64]
        plain[pl.ds(8 + half, half), 0:64] = body[:, 64:128]
        plain[pl.ds(0, 8), 0:64] = edge_ref[s, 0][:, 0:64] * keep_left
        plain[pl.ds(8 + rows, 8), 0:64] = edge_ref[s, 1][:, 0:64] * keep_right
        pairs[...] = plain[pl.ds(0, rows + 16), :] + pltpu.roll(
            plain[pl.ds(1, rows + 16), :], 64, axis=1
        )
        for m in range(4):
            lanes = slice(128 * m, 128 * m + 128)
            cols[pl.ds(s * rows, rows), lanes] = pairs[pl.ds(5 + 2 * m, rows), :].astype(jnp.bfloat16)
            rims[pl.ds(2 * s, 1), lanes] = pairs[pl.ds(4 + 2 * m, 1), :]
            rims[pl.ds(2 * s + 1, 1), lanes] = pairs[pl.ds(5 + 2 * m + rows, 1), :]
    cols[pl.ds(total, 16), :] = rims[...].astype(jnp.bfloat16)
    get_conv.wait()

    @pl.loop(0, act.shape[1] // 256)
    def _(n):
        lanes = pl.ds(pl.multiple_of(n * 256, 256), 256)
        alpha = alpha_ref[:, lanes]
        freq = alpha * PI_INV
        inv = 1.0 / alpha
        weight = conv_w[:, lanes]
        for part, size in [(s * rows, rows) for s in range(SEQS)] + [(total, 16)]:
            value = jnp.dot(
                cols[pl.ds(part, size), :], weight, preferred_element_type=jnp.float32
            )
            act[pl.ds(part, size), lanes] = snake(value, freq, inv).astype(jnp.bfloat16)

    line = lax.broadcasted_iota(jnp.int32, (16, 1), 0)
    gone = jnp.where(line % 2 == 0, keep_left, keep_right)
    edge_act = act[pl.ds(total, 16), :].astype(jnp.float32) * gone
    act[pl.ds(total, 16), :] = edge_act.astype(jnp.bfloat16)
    get_up.wait()

    for q in range(4):
        r = 2 * q
        tap = (r + 12) % 16
        near = jnp.concatenate([up_w[r + 4], up_w[r + 5]], axis=1)
        far = jnp.concatenate([up_w[tap], up_w[tap + 1]], axis=1)
        rim = jnp.dot(act[pl.ds(total, 16), :], far, preferred_element_type=jnp.float32)
        for s in range(SEQS):
            block = act[pl.ds(s * rows, rows), :]
            here[...] = jnp.dot(block, near, preferred_element_type=jnp.float32)
            other[pl.ds(8, rows), :] = jnp.dot(block, far, preferred_element_type=jnp.float32)
            if q < 2:
                other[pl.ds(7, 1), :] = rim[2 * s : 2 * s + 1]
                shifted = other[pl.ds(7, rows), :]
            else:
                other[pl.ds(8 + rows, 1), :] = rim[2 * s + 1 : 2 * s + 2]
                shifted = other[pl.ds(9, rows), :]
            both = here[...] + shifted
            tile[s, pl.ds(r, rows, stride=8), :] = both[:, 0:128]
            tile[s, pl.ds(r + 1, rows, stride=8), :] = both[:, 128:256]
    puts = [
        pltpu.make_async_copy(tile.at[s], out_hbm.at[s], out_sems.at[s]) for s in range(SEQS)
    ]
    for put in puts:
        put.start()
    for put in puts:
        put.wait()


def decode(main, edges, in_conv, snake_first, first_up):
    channels = in_conv.shape[2]
    rows = main.shape[1] * 2
    total = SEQS * rows + 16
    vmem = pl.BlockSpec(memory_space=pltpu.VMEM)
    anywhere = pl.BlockSpec(memory_space=pltpu.HBM)
    return pl.pallas_call(
        decode_kernel,
        out_shape=jax.ShapeDtypeStruct((SEQS, rows * 8, first_up.shape[2]), jnp.float32),
        in_specs=[vmem, vmem, vmem, anywhere, anywhere],
        out_specs=anywhere,
        scratch_shapes=[
            pltpu.VMEM((rows + 24, 128), jnp.float32),
            pltpu.VMEM((rows + 16, 128), jnp.float32),
            pltpu.VMEM((total, 512), jnp.bfloat16),
            pltpu.VMEM((16, 512), jnp.float32),
            pltpu.VMEM((8, 128), jnp.float32),
            pltpu.VMEM((total, channels), jnp.bfloat16),
            pltpu.VMEM((rows, 256), jnp.float32),
            pltpu.VMEM((rows + 16, 256), jnp.float32),
            pltpu.VMEM((SEQS, rows * 8, first_up.shape[2]), jnp.float32),
            pltpu.VMEM((512, channels), jnp.bfloat16),
            pltpu.VMEM(first_up.shape, jnp.bfloat16),
            pltpu.SemaphoreType.DMA((2,)),
            pltpu.SemaphoreType.DMA((SEQS,)),
        ],
        compiler_params=pltpu.CompilerParams(vmem_limit_bytes=63 << 20),
        cost_estimate=pl.CostEstimate(flops=11 * 10**9, bytes_accessed=16 << 20, transcendentals=0),
        name="decode",
    )(
        main,
        edges,
        snake_first[None, :],
        in_conv.reshape(-1, channels),
        first_up,
    )


def local(
    frames,
    expert_ids,
    gate_weights,
    up_weight,
    down_weight,
    out_weight,
    in_conv,
    snake_first,
    first_up,
):
    main, edges = experts(
        frames, expert_ids.T, gate_weights.T, out_weight.T, up_weight, down_weight
    )
    return decode(main, edges, in_conv, snake_first, first_up)


def solution(mesh):
    placed = (
        P(("seg", "expert"), None),
        P(("seg", "expert"), None),
        P(("seg", "expert"), None),
        P("expert", None, None),
        P("expert", None, None),
        P(),
        P(),
        P(),
        P(None, None, "seg"),
    )
    return jax.shard_map(
        local, mesh=mesh, in_specs=placed, out_specs=P(None, "expert", "seg"), check_vma=False
    )
```

```python
import jax
import jax.numpy as jnp
from jax import lax
from jax.experimental import pallas as pl
from jax.experimental.pallas import tpu as pltpu
from jax.sharding import PartitionSpec as P

SIN2 = (
    9.869604110717773,
    -32.469669342041016,
    42.727195739746094,
    -30.101465225219727,
    13.05009937286377,
    -3.3565926551818848,
)
PI_INV = 0.3183098861837907
SEQS = 4
SIDE = 4


def snake(values, freq, inv_alpha):
    turns = values * freq
    frac = turns - jnp.round(turns)
    t = frac * frac
    q = jnp.float32(SIN2[5])
    for coef in SIN2[4::-1]:
        q = q * t + coef
    return values + jnp.minimum(q * t, 1.0) * inv_alpha


OFFSETS = [
    (dx, (dx - shift) % SIDE, dc)
    for shift in (0, 1, 3, 2)
    for dc in range(2)
    for dx in range(SIDE)
]
WAVE = 8
WAVES = tuple((lo, lo + WAVE) for lo in range(0, len(OFFSETS), WAVE))
MESH = pl.DeviceIdType.MESH


def gelu(v):
    return 0.5 * v * (1.0 + jnp.tanh(0.7978845608 * (v + 0.044715 * v * v * v)))


def expert_kernel(
    frames_hbm, ids_hbm, gates_hbm, proj_hbm, up_hbm, down_hbm,
    main_ref, edge_ref,
    frames, ids, gates, proj, ranks, send, recv, rows_in, hidden, up_w, down_w, proj_w, table,
    picks, base, answer, returned, packed, ends, main_buf, edge_buf,
    w_sems, self_sem, out_s, out_r, back_s, back_r, main_s, main_r, end_s, end_r,
):
    expert = lax.axis_index("expert")
    seg = lax.axis_index("seg")
    x, z, core = expert // (2 * SIDE), (expert // 2) % SIDE, expert % 2

    def toward(step):
        dx, dz, dc = step
        return (((x + dx) % SIDE) * SIDE + (z + dz) % SIDE) * 2 + (core + dc) % 2

    def away(step):
        dx, dz, dc = step
        return (((x + SIDE - dx) % SIDE) * SIDE + (z + SIDE - dz) % SIDE) * 2 + (core + dc) % 2

    count = len(OFFSETS)
    sides = ((expert + 1) % count, (expert + count - 1) % count)
    barrier = pltpu.get_barrier_semaphore()
    for step in OFFSETS[1:]:
        pl.semaphore_signal(barrier, inc=1, device_id={"expert": toward(step)}, device_id_type=MESH)
    for ds in range(1, SEQS):
        for to in (expert,) + sides:
            pl.semaphore_signal(
                barrier,
                inc=1,
                device_id={"seg": (seg + ds) % SEQS, "expert": to},
                device_id_type=MESH,
            )
    gets = [
        pltpu.make_async_copy(src, dst, w_sems.at[k])
        for k, (src, dst) in enumerate(
            [
                (ids_hbm, ids), (frames_hbm, frames), (gates_hbm, gates), (proj_hbm, proj),
                (up_hbm, up_w), (down_hbm, down_w),
            ]
        )
    ]
    for get in gets:
        get.start()

    tokens, dim = frames.shape
    slots = recv.shape[1]
    gets[0].wait()
    name = lax.broadcasted_iota(jnp.int32, (count, tokens), 0)
    named = (ids[0:1, :] == name) | (ids[1:2, :] == name)
    line = lax.broadcasted_iota(jnp.int32, (tokens, tokens), 0)
    across = lax.broadcasted_iota(jnp.int32, (tokens, tokens), 1)
    earlier = jnp.where(line < across, 1.0, 0.0).astype(jnp.bfloat16)
    rank = jnp.dot(
        jnp.where(named, 1.0, 0.0).astype(jnp.bfloat16), earlier, preferred_element_type=jnp.float32
    )
    ranks[...] = jnp.where(named, rank, -1.0)
    gets[1].wait()
    slot = lax.broadcasted_iota(jnp.int32, (slots, 1), 0).astype(jnp.float32)

    def pack(lo, hi):
        rows = [
            jnp.where(ranks[pl.ds(toward(OFFSETS[i]), 1), :] == slot, 1.0, 0.0) for i in range(lo, hi)
        ]
        chosen = jnp.concatenate(rows, axis=0).astype(jnp.bfloat16)
        for n in range(dim // 512):
            lanes = slice(512 * n, 512 * n + 512)
            value = jnp.dot(chosen, frames[:, lanes], preferred_element_type=jnp.float32)
            send[lo:hi, :, lanes] = value.astype(jnp.bfloat16).reshape(hi - lo, slots, 512)

    outs = [None] * count

    def dispatch(lo, hi):
        for i in range(lo, hi):
            if i == 0:
                outs[i] = pltpu.make_async_copy(send.at[0], recv.at[0], self_sem)
            else:
                outs[i] = pltpu.make_async_remote_copy(
                    src_ref=send.at[i],
                    dst_ref=recv.at[i],
                    send_sem=out_s.at[i],
                    recv_sem=out_r.at[i],
                    device_id={"expert": toward(OFFSETS[i])},
                    device_id_type=MESH,
                )
            outs[i].start()

    pack(*WAVES[0])
    pl.semaphore_wait(barrier, count - 1 + 3 * (SEQS - 1))
    dispatch(*WAVES[0])
    pack(*WAVES[1])
    dispatch(*WAVES[1])
    for wave in WAVES[2:]:
        pack(*wave)

    gets[2].wait()
    gets[3].wait()
    lat = proj.shape[0]
    proj_w[0:lat, :] = proj[...]
    proj_w[lat : 2 * lat, :] = proj[...]
    base[...] = lax.dot_general(
        frames[...], proj_w[...], (((1,), (1,)), ((), ())), preferred_element_type=jnp.float32
    )
    table[...] = jnp.zeros_like(table)
    table[0:2, :] = ids[...].astype(jnp.float32)
    table[8:10, :] = gates[...]
    turned = jnp.transpose(table[...])
    choice = [turned[:, 0:1], turned[:, 1:2]]
    gate = [turned[:, 8:9], turned[:, 9:10]]
    lane = lax.broadcasted_iota(jnp.int32, (tokens, 128), 1).astype(jnp.float32)
    hits = [lane == choice[0], lane == choice[1]]
    named = jnp.where(hits[0] | hits[1], 1.0, 0.0).astype(jnp.bfloat16)
    before = jnp.where(across < line, 1.0, 0.0).astype(jnp.bfloat16)
    rank = jnp.dot(before, named, preferred_element_type=jnp.float32)
    spot = lax.broadcasted_iota(jnp.int32, (tokens, count * slots), 1).astype(jnp.float32)
    for c in range(2):
        dest = choice[c] * slots + jnp.sum(
            jnp.where(hits[c], rank, 0.0), axis=1, keepdims=True
        )
        picks[pl.ds(c * tokens, tokens), :] = jnp.where(spot == dest, 1.0, 0.0).astype(jnp.bfloat16)

    gets[4].wait()
    gets[5].wait()
    backs = [None] * count
    first = lax.broadcasted_iota(jnp.int32, (1, 2 * lat), 1) < lat
    width = 512
    for turn, (lo, hi) in enumerate(WAVES):
        for i in range(lo, hi):
            if i == 0:
                outs[i].wait()
            else:
                outs[i].wait_recv()
        if turn + 2 < len(WAVES):
            dispatch(*WAVES[turn + 2])
        size = (hi - lo) * slots
        rows_in[0:size, :] = recv[lo:hi].reshape(size, recv.shape[2])

        @pl.loop(0, hidden.shape[1] // width)
        def _(n):
            lanes = pl.ds(pl.multiple_of(n * width, width), width)
            value = jnp.dot(
                rows_in[0:size, :], up_w[0, :, lanes], preferred_element_type=jnp.float32
            )
            hidden[0:size, lanes] = gelu(value).astype(jnp.bfloat16)

        sent = jnp.zeros((size, 2 * lat), jnp.float32)
        for n in range(rows_in.shape[1] // width):
            lanes = slice(n * width, n * width + width)
            value = jnp.dot(
                hidden[0:size, :], down_w[0, :, lanes], preferred_element_type=jnp.float32
            ).astype(jnp.bfloat16)
            sent = sent + lax.dot_general(
                value, proj_w[:, lanes], (((1,), (1,)), ((), ())), preferred_element_type=jnp.float32
            )
        high = sent.astype(jnp.bfloat16).astype(jnp.float32)
        split = jnp.where(first, high, sent - high).astype(jnp.bfloat16)
        answer[lo:hi] = split.reshape(hi - lo, slots, 2 * lat)
        for i in range(lo, hi):
            if i == 0:
                backs[i] = pltpu.make_async_copy(answer.at[i], returned.at[expert], back_r.at[i])
            else:
                backs[i] = pltpu.make_async_remote_copy(
                    src_ref=answer.at[i],
                    dst_ref=returned.at[expert],
                    send_sem=back_s.at[i],
                    recv_sem=back_r.at[i],
                    device_id={"expert": away(OFFSETS[i])},
                    device_id_type=MESH,
                )
            backs[i].start()

    for i in range(count):
        if i == 0:
            backs[i].wait()
        else:
            pltpu.make_async_remote_copy(
                src_ref=answer.at[i],
                dst_ref=returned.at[toward(OFFSETS[i])],
                send_sem=back_s.at[i],
                recv_sem=back_r.at[i],
                device_id={"expert": away(OFFSETS[i])},
                device_id_type=MESH,
            ).wait_recv()
    got = jnp.dot(
        picks[...],
        returned[...].reshape(count * slots, 2 * lat),
        preferred_element_type=jnp.float32,
    )
    got = got + pltpu.roll(got, lat, axis=1)
    latent = base[...] + gate[0] * got[0:tokens] + gate[1] * got[tokens:]
    latent = latent.astype(jnp.bfloat16).astype(jnp.float32)
    half = tokens // 2
    packed[...] = jnp.where(first, latent[0:half], latent[half:]).astype(jnp.bfloat16)
    ends[0] = latent[tokens - 8 :]
    ends[1] = latent[0:8]

    sends = []
    for side in range(2):
        for ds in range(SEQS):
            k = side * SEQS + ds
            copy = pltpu.make_async_remote_copy(
                src_ref=ends.at[side],
                dst_ref=edge_buf.at[seg, side],
                send_sem=end_s.at[k],
                recv_sem=end_r.at[k],
                device_id={"seg": (seg + ds) % SEQS, "expert": sides[side]},
                device_id_type=MESH,
            )
            copy.start()
            sends.append((copy, edge_buf.at[(seg + SEQS - ds) % SEQS, side], end_s.at[k], end_r.at[k]))
    for ds in range(1, SEQS):
        copy = pltpu.make_async_remote_copy(
            src_ref=packed,
            dst_ref=main_buf.at[seg],
            send_sem=main_s.at[ds],
            recv_sem=main_r.at[ds],
            device_id={"seg": (seg + ds) % SEQS, "expert": expert},
            device_id_type=MESH,
        )
        copy.start()
        sends.append((copy, main_buf.at[(seg + SEQS - ds) % SEQS], main_s.at[ds], main_r.at[ds]))
    main_buf[seg] = packed[...]
    for k, (copy, landing, ss, rs) in enumerate(sends):
        pltpu.make_async_remote_copy(
            src_ref=ends.at[0] if k < 2 * SEQS else packed,
            dst_ref=landing,
            send_sem=ss,
            recv_sem=rs,
            device_id={"seg": (seg + 1) % SEQS, "expert": expert},
            device_id_type=MESH,
        ).wait_recv()
    main_ref[...] = main_buf[...]
    edge_ref[...] = edge_buf[...]
    for copy in outs[1:] + backs[1:] + [entry[0] for entry in sends]:
        copy.wait_send()


def experts(frames, ids, gates, proj, up_weight, down_weight):
    tokens, dim = frames.shape
    count = len(OFFSETS)
    slots = 3 * tokens // count
    hid = up_weight.shape[2]
    lat = proj.shape[0]
    vmem = pl.BlockSpec(memory_space=pltpu.VMEM)
    anywhere = pl.BlockSpec(memory_space=pltpu.HBM)
    bf16, f32 = jnp.bfloat16, jnp.float32
    top = WAVE * slots
    sems = lambda *shape: pltpu.SemaphoreType.DMA(shape)
    return pl.pallas_call(
        expert_kernel,
        out_shape=(
            jax.ShapeDtypeStruct((SEQS, tokens // 2, 2 * lat), bf16),
            jax.ShapeDtypeStruct((SEQS, 2, 8, 2 * lat), f32),
        ),
        in_specs=[anywhere] * 6,
        out_specs=(vmem, vmem),
        scratch_shapes=[
            pltpu.VMEM(frames.shape, bf16),
            pltpu.VMEM(ids.shape, jnp.int32),
            pltpu.VMEM(gates.shape, f32),
            pltpu.VMEM(proj.shape, bf16),
            pltpu.VMEM((count, tokens), f32),
            pltpu.VMEM((count, slots, dim), bf16),
            pltpu.VMEM((count, slots, dim), bf16),
            pltpu.VMEM((top, dim), bf16),
            pltpu.VMEM((top, hid), bf16),
            pltpu.VMEM(up_weight.shape, bf16),
            pltpu.VMEM(down_weight.shape, bf16),
            pltpu.VMEM((2 * lat, dim), bf16),
            pltpu.VMEM((128, tokens), f32),
            pltpu.VMEM((2 * tokens, count * slots), bf16),
            pltpu.VMEM((tokens, 2 * lat), f32),
            pltpu.VMEM((count, slots, 2 * lat), bf16),
            pltpu.VMEM((count, slots, 2 * lat), bf16),
            pltpu.VMEM((tokens // 2, 2 * lat), bf16),
            pltpu.VMEM((2, 8, 2 * lat), f32),
            pltpu.VMEM((SEQS, tokens // 2, 2 * lat), bf16),
            pltpu.VMEM((SEQS, 2, 8, 2 * lat), f32),
            sems(6), sems(), sems(count), sems(count), sems(count), sems(count),
            sems(SEQS), sems(SEQS), sems(2 * SEQS), sems(2 * SEQS),
        ],
        compiler_params=pltpu.CompilerParams(
            collective_id=0, has_side_effects=True, vmem_limit_bytes=63 << 20
        ),
        cost_estimate=pl.CostEstimate(
            flops=10 * 10**9, bytes_accessed=16 << 20, transcendentals=0
        ),
        name="experts",
    )(frames, ids, gates, proj, up_weight, down_weight)


def decode_kernel(main_ref, edge_ref, alpha_ref, conv_hbm, up_hbm, out_hbm, *scratch):
    plain, pairs, shifted, tile, conv_w, up_w, in_sems, out_sems = scratch[:8]
    cols, act = scratch[8 : 8 + SEQS], scratch[8 + SEQS :]
    rows = main_ref.shape[1] * 2
    height = rows + 16
    get_conv = pltpu.make_async_copy(conv_hbm, conv_w.at[pl.ds(0, 448)], in_sems.at[0])
    get_conv.start()
    get_up = pltpu.make_async_copy(up_hbm, up_w, in_sems.at[1])
    get_up.start()
    slab = lax.axis_index("expert")
    keep_left = jnp.where(slab == 0, 0.0, 1.0)
    keep_right = jnp.where(slab == lax.axis_size("expert") - 1, 0.0, 1.0)
    conv_w[pl.ds(448, 64), :] = jnp.zeros((64, conv_w.shape[1]), jnp.bfloat16)
    plain[...] = jnp.zeros_like(plain)

    for s in range(SEQS):
        body = main_ref[s].astype(jnp.float32)
        half = rows // 2
        plain[pl.ds(8, 8), 0:64] = edge_ref[s, 0][:, 0:64] * keep_left
        plain[pl.ds(16, half), 0:64] = body[:, 0:64]
        plain[pl.ds(16 + half, half), 0:64] = body[:, 64:128]
        plain[pl.ds(16 + rows, 8), 0:64] = edge_ref[s, 1][:, 0:64] * keep_right
        size = pairs.shape[0]
        pairs[...] = plain[pl.ds(0, size), :] + pltpu.roll(plain[pl.ds(1, size), :], 64, axis=1)
        for m in range(4):
            cols[s][:, 128 * m : 128 * m + 128] = pairs[pl.ds(5 + 2 * m, height), :].astype(
                jnp.bfloat16
            )
    get_conv.wait()

    def activate(s, lanes):
        alpha = alpha_ref[:, lanes]
        value = jnp.dot(cols[s][...], conv_w[:, lanes], preferred_element_type=jnp.float32)
        value = snake(value, alpha * PI_INV, 1.0 / alpha)
        value = jnp.concatenate(
            [value[0:8] * keep_left, value[8 : 8 + rows], value[8 + rows :] * keep_right], axis=0
        )
        act[s][:, lanes] = value.astype(jnp.bfloat16)

    @pl.loop(0, conv_w.shape[1] // 256)
    def _(n):
        activate(0, pl.ds(pl.multiple_of(n * 256, 256), 256))

    get_up.wait()
    puts = []
    for s in range(SEQS):
        for q in range(4):
            r = 2 * q
            tap = (r + 12) % 16
            near = jnp.concatenate([up_w[r + 4], up_w[r + 5]], axis=1)
            far = jnp.concatenate([up_w[tap], up_w[tap + 1]], axis=1)
            buf = shifted.at[q % 2]
            buf[...] = jnp.dot(act[s][...], far, preferred_element_type=jnp.float32)
            if s + 1 < SEQS:
                activate(s + 1, slice(512 * q, 512 * q + 256))
            both = jnp.dot(act[s][...], near, preferred_element_type=jnp.float32)[8 : 8 + rows]
            both = both + buf[pl.ds(7 if q < 2 else 9, rows), :]
            if s + 1 < SEQS:
                activate(s + 1, slice(512 * q + 256, 512 * q + 512))
            tile[s, pl.ds(r, rows, stride=8), :] = both[:, 0:128]
            tile[s, pl.ds(r + 1, rows, stride=8), :] = both[:, 128:256]
        puts.append(pltpu.make_async_copy(tile.at[s], out_hbm.at[s], out_sems.at[s]))
        puts[s].start()
    for put in puts:
        put.wait()


def decode(main, edges, in_conv, snake_first, first_up):
    channels = in_conv.shape[2]
    rows = main.shape[1] * 2
    vmem = pl.BlockSpec(memory_space=pltpu.VMEM)
    anywhere = pl.BlockSpec(memory_space=pltpu.HBM)
    return pl.pallas_call(
        decode_kernel,
        out_shape=jax.ShapeDtypeStruct((SEQS, rows * 8, first_up.shape[2]), jnp.float32),
        in_specs=[vmem, vmem, vmem, anywhere, anywhere],
        out_specs=anywhere,
        scratch_shapes=[
            pltpu.VMEM((rows + 48, 128), jnp.float32),
            pltpu.VMEM((rows + 32, 128), jnp.float32),
            pltpu.VMEM((2, rows + 16, 256), jnp.float32),
            pltpu.VMEM((SEQS, rows * 8, first_up.shape[2]), jnp.float32),
            pltpu.VMEM((512, channels), jnp.bfloat16),
            pltpu.VMEM(first_up.shape, jnp.bfloat16),
            pltpu.SemaphoreType.DMA((2,)),
            pltpu.SemaphoreType.DMA((SEQS,)),
        ]
        + [pltpu.VMEM((rows + 16, 512), jnp.bfloat16)] * SEQS
        + [pltpu.VMEM((rows + 16, channels), jnp.bfloat16)] * SEQS,
        compiler_params=pltpu.CompilerParams(vmem_limit_bytes=63 << 20),
        cost_estimate=pl.CostEstimate(flops=11 * 10**9, bytes_accessed=16 << 20, transcendentals=0),
        name="decode",
    )(main, edges, snake_first[None, :], in_conv.reshape(-1, channels), first_up)


def local(
    frames,
    expert_ids,
    gate_weights,
    up_weight,
    down_weight,
    out_weight,
    in_conv,
    snake_first,
    first_up,
):
    main, edges = experts(
        frames, expert_ids.T, gate_weights.T, out_weight.T, up_weight, down_weight
    )
    return decode(main, edges, in_conv, snake_first, first_up)


def solution(mesh):
    placed = (
        P(("seg", "expert"), None),
        P(("seg", "expert"), None),
        P(("seg", "expert"), None),
        P("expert", None, None),
        P("expert", None, None),
        P(),
        P(),
        P(),
        P(None, None, "seg"),
    )
    return jax.shard_map(
        local, mesh=mesh, in_specs=placed, out_specs=P(None, "expert", "seg"), check_vma=False
    )
```
